32 devices in a mesh: section: 2 (over core), dp: 4 (over z), tensor: 4 (over y, x).
Axes of the slice: x: 2, y: 2, z: 4, core: 2. Of those that a mesh axis runs over, the one named last changes fastest.
Arguments:
- inputs: bfloat16 [2, 4096, 768], P(None, ('dp', 'tensor')), may hold values from -6 to 6
- lengths: int32 [2, 4], P(None, 'dp'), may hold values from 1 to 1024, 2457 in all within a row
- cotangent: bfloat16 [2, 4096, 768], P(None, ('dp', 'tensor')), may hold values from -6 to 6
- w_query: bfloat16 [2, 768, 768], P('section', 'dp', 'tensor'), may hold values from -0.21875 to 0.21875
- w_key: bfloat16 [2, 768, 768], P('section', 'dp', 'tensor'), may hold values from -0.21875 to 0.21875
- w_value: bfloat16 [2, 768, 768], P('section', 'dp', 'tensor'), may hold values from -0.21875 to 0.21875
- w_out: bfloat16 [2, 768, 768], P('section', 'dp', 'tensor'), may hold values from -2 to 2
- w_gate: bfloat16 [2, 768, 1152], P('section', 'dp', 'tensor'), may hold values from -0.21875 to 0.21875
- w_up: bfloat16 [2, 768, 1152], P('section', 'dp', 'tensor'), may hold values from -0.21875 to 0.21875
- w_down: bfloat16 [2, 768, 1152], P('section', 'dp', 'tensor'), may hold values from -0.375 to 0.375
- norm_gains: bfloat16 [2, 768, 2], P('section', 'dp'), may hold values from 0.5 to 1.5
Outputs:
- activations: bfloat16 [2, 2, 4096, 768], P('section', None, ('dp', 'tensor'))
- input_grads: bfloat16 [2, 2, 4096, 768], P('section', None, ('dp', 'tensor'))
- grad_query: float32 [2, 768, 768], P('section', 'dp', 'tensor')
- grad_key: float32 [2, 768, 768], P('section', 'dp', 'tensor')
- grad_value: float32 [2, 768, 768], P('section', 'dp', 'tensor')
- grad_out: float32 [2, 768, 768], P('section', 'dp', 'tensor')
- grad_gate: float32 [2, 768, 1152], P('section', 'dp', 'tensor')
- grad_up: float32 [2, 768, 1152], P('section', 'dp', 'tensor')
- grad_down: float32 [2, 768, 1152], P('section', 'dp', 'tensor')
- grad_gains: float32 [2, 768, 2], P('section', 'dp')
The draws below stay inside these ranges and needn't reach their ends.
Inputs may be any that keep to these rules, and one draw needn't show every extreme that they name: Each micro-batch's lengths sum to 2457 and their largest is exactly 1024; a sequence occupies the first lengths[m, d] positions of its 1024 rows, the rest is padding.
All inputs are finite; a program needn't handle non-finite values. No bound on the sum of `lengths` on one device may be relied on, other than what follows from the above.
Results may differ from the reference program's by a relative error of at most 0.03.
Values may be sent and summed in bfloat16 or wider, within the bound.
No kernel may reach another device: no remote copies, remote signals or barrier semaphores. Data moves between devices by JAX's collectives and lax.ppermute only.
A program may use at most 192 MiB of HBM per device.

```python
import math
import jax
import jax.numpy as jnp
import numpy as np
from jax import lax

D = 768
HEADS = 12
FF = 1152
HEAD = 64
WINDOW = 128
SLOT = 1024
MICRO = 2
N_DP = 4


def steps_of(key, dims, shards, smallest, largest):
    factor_of, own = 1.0, jax.random.fold_in(key, 6)
    for axis_at, blocks in shards:
        draws = jnp.exp(jax.random.uniform(jax.random.fold_in(own, axis_at), (blocks,), jnp.float32, smallest / len(shards), largest / len(shards)))
        factor_of = factor_of * jnp.repeat(draws, dims[axis_at] // blocks).reshape([-1 if axis == axis_at else 1 for axis in range(len(dims))])
    return factor_of


def profile(number_of, total, bound, lean):
    weights = [(1 << 20) // math.isqrt(grade ** lean) + 1 for grade in range(2, number_of + 1)]
    surplus, given = total - bound - (number_of - 1), [1] * (number_of - 1)
    while surplus > 0:
        free = [i for i in range(number_of - 1) if given[i] < bound]
        mass, left = sum([weights[i] for i in free]), surplus
        for i in free:
            more = min(bound - given[i], max(1, left * weights[i] // mass), surplus)
            given[i] = given[i] + more
            surplus = surplus - more
    return np.array([bound] + given)


def uneven(rng, amount, total, bound, skew):
    if amount == 2:
        one = jax.random.randint(rng, (), max(1, total - bound), min(bound, total - 1) + 1)
        return jnp.stack([one, total - one])
    sizes = jnp.asarray(profile(amount, total, bound, skew), jnp.int32)
    pairs = (amount - 1) // 2
    donor, receiver = sizes[1:1 + 2 * pairs:2], sizes[2:2 + 2 * pairs:2]
    margin = jnp.minimum(donor - 1, bound - receiver)
    shifted = jax.random.randint(jax.random.fold_in(rng, 1), (pairs,), 0, 1 << 20) % (margin + 1)
    sizes = sizes.at[1:1 + 2 * pairs:2].set(donor - shifted).at[2:2 + 2 * pairs:2].set(receiver + shifted)
    return sizes[jax.random.permutation(jax.random.fold_in(rng, 2), amount)]


def gaussian(stream_key, extent, width, bound, pieces=(), kind=jnp.bfloat16):
    factor_of = steps_of(stream_key, extent, pieces, -0.22, 0.18) if pieces else 1.0
    drawn = jax.random.normal(stream_key, extent, jnp.float32) * width * factor_of
    return jnp.minimum(jnp.maximum(drawn, -bound), bound).astype(kind)


def setup_inputs(seed: int = 0) -> dict:
    seeds = jax.random.split(jax.random.key(seed), 12)
    inputs = gaussian(seeds[0], (MICRO, N_DP * SLOT, D), 1.0, 6.0, ((1, 16),))
    lengths = jax.vmap(lambda own: uneven(own, N_DP, N_DP * SLOT * 3 // 5, SLOT, 2))(jax.random.split(seeds[1], MICRO)).reshape((MICRO, N_DP)).astype(jnp.int32)
    cotangent = gaussian(seeds[2], (MICRO, N_DP * SLOT, D), 1.0, 6.0, ((1, 16),))
    w_query = gaussian(seeds[3], (2, D, D), D ** -0.5, 0.21875, ((0, 2), (1, 4), (2, 4)))
    w_key = gaussian(seeds[4], (2, D, D), D ** -0.5, 0.21875, ((0, 2), (1, 4), (2, 4)))
    w_value = gaussian(seeds[5], (2, D, D), D ** -0.5, 0.21875, ((0, 2), (1, 4), (2, 4)))
    w_out = gaussian(seeds[6], (2, D, D), (HEAD // 8) ** -0.5, 2.0, ((0, 2), (1, 4), (2, 4)))
    w_gate = gaussian(seeds[7], (2, D, FF), D ** -0.5, 0.21875, ((0, 2), (1, 4), (2, 4)))
    w_up = gaussian(seeds[8], (2, D, FF), D ** -0.5, 0.21875, ((0, 2), (1, 4), (2, 4)))
    w_down = gaussian(seeds[9], (2, D, FF), (FF // 4) ** -0.5, 0.375, ((0, 2), (1, 4), (2, 4)))
    norm_gains = jnp.clip(1.0 + 0.1 * jax.random.normal(seeds[10], (2, D, 2), jnp.float32), 0.5, 1.5).astype(jnp.bfloat16)
    return {"inputs": inputs, "lengths": lengths, "cotangent": cotangent, "w_query": w_query, "w_key": w_key, "w_value": w_value, "w_out": w_out, "w_gate": w_gate, "w_up": w_up, "w_down": w_down, "norm_gains": norm_gains}


HIGHEST = lax.Precision.HIGHEST
EPSILON = 1e-05

@jax.custom_vjp
def low(v):
    return lax.optimization_barrier(v.astype(jnp.bfloat16)).astype(jnp.float32)

@jax.custom_vjp
def low_back(v):
    return v

def low_keep(v):
    return (low(v), None)

def low_pass(kept, grad):
    return (grad,)

def back_keep(v):
    return (v, None)

def back_low(kept, grad):
    return (low(grad),)
low.defvjp(low_keep, low_pass)
low_back.defvjp(back_keep, back_low)

def layer_norm(rows, gain):
    centre = rows - lax.optimization_barrier(jnp.mean(rows, axis=-1, keepdims=True))
    variance = lax.optimization_barrier(jnp.mean(centre * centre, axis=-1, keepdims=True))
    return centre * lax.rsqrt(variance + EPSILON) * gain

def rotary_tables(count, theta):
    position = jnp.arange(count, dtype=jnp.float32)[:, None]
    index = jnp.arange(HEAD // 2, dtype=jnp.float32)[None, :]
    inverse = jnp.exp(-jnp.log(theta) * (2.0 * index / HEAD))
    angle = position * inverse
    cosine = jnp.concatenate([jnp.cos(angle), jnp.cos(angle)], axis=1)[:, None, :]
    sine = jnp.concatenate([jnp.sin(angle), jnp.sin(angle)], axis=1)[:, None, :]
    return (cosine, sine)

def rotate(heads, cosine, sine):
    half = HEAD // 2
    turned = jnp.concatenate([-heads[..., half:], heads[..., :half]], axis=-1)
    return heads * cosine + turned * sine

def visible(count, half_window, length):
    rows = jnp.arange(count, dtype=jnp.int32)[:, None]
    columns = jnp.arange(count, dtype=jnp.int32)[None, :]
    near = (jnp.abs(rows - columns) <= half_window) & (columns < length)
    return near | (rows == columns)

def one_layer(resid, params, half_window, theta, length):
    w_query, w_key, w_value, w_out, w_gate, w_up, w_down, gains = params
    count = resid.shape[0]
    normed = low(layer_norm(resid, gains[:, 0]))
    query = jnp.dot(normed, w_query, precision=HIGHEST)
    key = jnp.dot(normed, w_key, precision=HIGHEST)
    value = jnp.dot(normed, w_value, precision=HIGHEST)
    cosine, sine = rotary_tables(count, theta)
    q_rot = low(rotate(low_back(query).reshape(count, HEADS, HEAD), cosine, sine))
    k_rot = low(rotate(low_back(key).reshape(count, HEADS, HEAD), cosine, sine))
    v_low = low(low_back(value)).reshape(count, HEADS, HEAD)
    scores = low_back(jnp.einsum('qhd,khd->hqk', q_rot, k_rot, precision=HIGHEST) * HEAD ** (-0.5))
    allowed = visible(count, half_window, length)[None]
    probs = jax.nn.softmax(jnp.where(allowed, scores, -1e+30), axis=-1)
    attended = jnp.einsum('hqk,khd->qhd', low(probs), v_low, precision=HIGHEST).reshape(count, D)
    attended = low(low_back(attended))
    mixed = resid + low_back(jnp.dot(attended, w_out.T, precision=HIGHEST))
    normed_two = low(layer_norm(mixed, gains[:, 1]))
    gate = low_back(jnp.dot(normed_two, w_gate, precision=HIGHEST))
    upper = low_back(jnp.dot(normed_two, w_up, precision=HIGHEST))
    hidden = low(jax.nn.gelu(gate, approximate=False) * upper)
    return mixed + low_back(jnp.dot(hidden, w_down.T, precision=HIGHEST))

def reference(inputs, lengths, cotangent, w_query, w_key, w_value, w_out, w_gate, w_up, w_down, norm_gains):
    count = MICRO * N_DP
    sequences = inputs.astype(jnp.float32).reshape(count, SLOT, D)
    seq_lengths = lengths.reshape(count).astype(jnp.int32)
    weights = tuple((w.astype(jnp.float32) for w in (w_query, w_key, w_value, w_out, w_gate, w_up, w_down, norm_gains)))
    probe = jnp.zeros_like(sequences)

    def forward(sequences, probe, weights):

        def per_sequence(item):
            sequence, extra, length = item
            first = tuple((w[0] for w in weights))
            second = tuple((w[1] for w in weights))
            middle = low_back(low(one_layer(sequence, first, WINDOW // 2, 10000.0, length))) + extra
            final = low(one_layer(middle, second, SLOT, 160000.0, length))
            return (middle, final)
        return lax.map(jax.checkpoint(per_sequence), (sequences, probe, seq_lengths))
    (middle, final), pull = jax.vjp(forward, sequences, probe, weights)
    top_grad = cotangent.astype(jnp.float32).reshape(count, SLOT, D)
    d_sequences, d_probe, d_weights = pull((jnp.zeros_like(middle), top_grad))
    shape = (MICRO, N_DP * SLOT, D)
    activations = jnp.stack([middle.reshape(shape), final.reshape(shape)]).astype(jnp.bfloat16)
    input_grads = jnp.stack([d_sequences.reshape(shape), d_probe.reshape(shape)]).astype(jnp.bfloat16)
    return (activations, input_grads, d_weights[0], d_weights[1], d_weights[2], d_weights[3], d_weights[4], d_weights[5], d_weights[6], d_weights[7])
```

```python
import functools

import jax
import jax.numpy as jnp
from jax import lax
from jax.experimental import pallas as pl
from jax.experimental.pallas import tpu as pltpu
from jax.sharding import PartitionSpec as P

HEAD = 64
HALF_WINDOW = 64
THETAS = (10000.0, 160000.0)
EPSILON = 1e-05
SCALE = HEAD ** (-0.5)
MASKED = -1e30
BF16 = jnp.bfloat16
F32 = jnp.float32
NT = (((1,), (1,)), ((), ()))


def layer_norm(rows, gain):
    centre = rows - jnp.mean(rows, axis=-1, keepdims=True)
    variance = jnp.mean(centre * centre, axis=-1, keepdims=True)
    return centre * lax.rsqrt(variance + EPSILON) * gain


def geglu(gate, upper):
    return jax.nn.gelu(gate, approximate=False) * upper


def exchange(value, by):
    count = lax.axis_size("tensor")
    return lax.ppermute(value, "tensor", [(i, i ^ by) for i in range(count)])


def gather_rows(rows):
    count = lax.axis_size("tensor")
    return jnp.concatenate([rows] + [exchange(rows, by) for by in range(1, count)], axis=0)


def scatter_rows(partial):
    count = lax.axis_size("tensor")
    own = partial.shape[0] // count
    total = partial[:own].astype(F32)
    for by in range(1, count):
        total = total + exchange(partial[by * own : (by + 1) * own], by).astype(F32)
    return total


def positions(own, devices):
    index = lax.axis_index("tensor")
    row = jnp.arange(own * devices, dtype=jnp.int32)
    return ((row // own) ^ index) * own + row % own


def rotary_tables(position, theta):
    index = jnp.arange(HEAD // 2, dtype=F32)[None, :]
    inverse = jnp.exp(-jnp.log(F32(theta)) * (2.0 * index / HEAD))
    angle = position.astype(F32)[:, None] * inverse
    cosine = jnp.cos(angle)
    sine = jnp.sin(angle)
    return (
        jnp.concatenate([cosine, cosine], axis=1),
        jnp.concatenate([sine, sine], axis=1),
    )


def turn(rows):
    half = HEAD // 2
    return jnp.concatenate([-rows[:, half:], rows[:, :half]], axis=1)


def neighbours(scalars, block, own, devices):
    index = scalars[0]
    place = index ^ block
    before = (jnp.maximum(place - 1, 0) ^ index) * own + own - HALF_WINDOW
    after = (jnp.minimum(place + 1, devices - 1) ^ index) * own
    return place, pl.multiple_of(before, HALF_WINDOW), pl.multiple_of(after, HALF_WINDOW)


def attend_kernel(scalars, qkv, cosine, sine, q3, k3, v3, out, lse, *, local, own, devices, heads):
    count = own * devices
    width = heads * HEAD
    length = scalars[1]
    for head in range(heads):
        at = head * HEAD
        for part, store in ((0, q3), (1, k3)):
            rows = qkv[:, part * width + at : part * width + at + HEAD]
            store[head] = (rows * cosine[...] + turn(rows) * sine[...]).astype(BF16)
        v3[head] = qkv[:, 2 * width + at : 2 * width + at + HEAD].astype(BF16)
    for head in range(heads):

        def step(block, carry):
            start = pl.multiple_of(block * own, own)
            query = q3[head, pl.ds(start, own), :]
            if local:
                place, before, after = neighbours(scalars, block, own, devices)
                key = jnp.concatenate(
                    [
                        k3[head, pl.ds(before, HALF_WINDOW), :],
                        k3[head, pl.ds(start, own), :],
                        k3[head, pl.ds(after, HALF_WINDOW), :],
                    ],
                    axis=0,
                )
                value = jnp.concatenate(
                    [
                        v3[head, pl.ds(before, HALF_WINDOW), :],
                        v3[head, pl.ds(start, own), :],
                        v3[head, pl.ds(after, HALF_WINDOW), :],
                    ],
                    axis=0,
                )
                span = own + 2 * HALF_WINDOW
                shape = (own, span)
                row = lax.broadcasted_iota(jnp.int32, shape, 0)
                column = lax.broadcasted_iota(jnp.int32, shape, 1) - HALF_WINDOW
                spot = column + place * own
                near = jnp.abs(row - column) <= HALF_WINDOW
                allowed = (near & (spot >= 0) & (spot < length)) | (row == column)
            else:
                key = k3[head]
                value = v3[head]
                shape = (own, count)
                row = lax.broadcasted_iota(jnp.int32, shape, 0) + start
                column = lax.broadcasted_iota(jnp.int32, shape, 1)
                spot = ((column // own) ^ scalars[0]) * own + column % own
                allowed = (spot < length) | (row == column)
            raw = lax.dot_general(query, key, NT, preferred_element_type=F32) * SCALE
            scores = jnp.where(allowed, raw, MASKED)
            highest = jnp.max(scores, axis=1, keepdims=True)
            lifted = jnp.exp(scores - highest)
            summed = jnp.sum(lifted, axis=1, keepdims=True)
            probs = (lifted / summed).astype(BF16)
            got = jnp.dot(probs, value, preferred_element_type=F32)
            out[pl.ds(start, own), head * HEAD : (head + 1) * HEAD] = got.astype(BF16)
            total = jnp.broadcast_to(highest + jnp.log(summed), (own, 128))
            lse[head, :, pl.ds(start, own)] = total.T[:8]
            return carry

        lax.fori_loop(0, devices, step, 0)


def attend(qkv, cosine, sine, scalars, local, own, devices, heads):
    count = own * devices
    split = jax.ShapeDtypeStruct((heads, count, HEAD), BF16)
    vmem = pl.BlockSpec(memory_space=pltpu.VMEM)
    return pl.pallas_call(
        functools.partial(attend_kernel, local=local, own=own, devices=devices, heads=heads),
        out_shape=(
            split,
            split,
            split,
            jax.ShapeDtypeStruct((count, heads * HEAD), BF16),
            jax.ShapeDtypeStruct((heads, 8, count), F32),
        ),
        in_specs=[pl.BlockSpec(memory_space=pltpu.SMEM), vmem, vmem, vmem],
        out_specs=(vmem, vmem, vmem, vmem, vmem),
        name="attend",
    )(scalars, qkv, cosine, sine)


def attend_back_kernel(
    scalars, q3, k3, v3, grad, lse, cosine, sine, out, dk, dv, *, local, own, devices, heads
):
    count = own * devices
    width = heads * HEAD
    length = scalars[1]
    for head in range(heads):
        dk[...] = jnp.zeros_like(dk)
        dv[...] = jnp.zeros_like(dv)

        def step(block, carry):
            start = pl.multiple_of(block * own, own)
            here = pl.ds(start, own)
            query = q3[head, here, :]
            upstream = grad[here, head * HEAD : (head + 1) * HEAD]
            if local:
                place, before, after = neighbours(scalars, block, own, devices)
                pieces = (
                    (pl.ds(before, HALF_WINDOW), 0, HALF_WINDOW),
                    (here, HALF_WINDOW, HALF_WINDOW + own),
                    (pl.ds(after, HALF_WINDOW), HALF_WINDOW + own, 2 * HALF_WINDOW + own),
                )
                key = jnp.concatenate([k3[head, piece, :] for piece, _, _ in pieces], axis=0)
                value = jnp.concatenate([v3[head, piece, :] for piece, _, _ in pieces], axis=0)
                shape = (own + 2 * HALF_WINDOW, own)
                row = lax.broadcasted_iota(jnp.int32, shape, 1)
                column = lax.broadcasted_iota(jnp.int32, shape, 0) - HALF_WINDOW
                spot = column + place * own
                near = jnp.abs(row - column) <= HALF_WINDOW
                allowed = (near & (spot >= 0) & (spot < length)) | (row == column)
            else:
                pieces = ((slice(None), 0, count),)
                key = k3[head]
                value = v3[head]
                shape = (count, own)
                row = lax.broadcasted_iota(jnp.int32, shape, 1) + start
                column = lax.broadcasted_iota(jnp.int32, shape, 0)
                spot = ((column // own) ^ scalars[0]) * own + column % own
                allowed = (spot < length) | (row == column)
            raw = lax.dot_general(key, query, NT, preferred_element_type=F32) * SCALE
            scores = jnp.where(allowed, raw, MASKED)
            probs = jnp.exp(scores - lse[head, 0:1, here])
            d_probs = lax.dot_general(value, upstream, NT, preferred_element_type=F32)
            weighted = jnp.sum(probs * d_probs, axis=0, keepdims=True)
            d_scores = (probs * (d_probs - weighted)).astype(BF16)
            d_key = jnp.dot(d_scores, query, preferred_element_type=F32) * SCALE
            d_value = jnp.dot(probs.astype(BF16), upstream, preferred_element_type=F32)
            for piece, low, high in pieces:
                dk[piece, :] += d_key[low:high]
                dv[piece, :] += d_value[low:high]
            d_query = jnp.dot(key.T, d_scores, preferred_element_type=F32).T * SCALE
            d_query = d_query * cosine[here, :] - turn(d_query) * sine[here, :]
            out[here, head * HEAD : (head + 1) * HEAD] = d_query.astype(BF16)
            return carry

        lax.fori_loop(0, devices, step, 0)
        at = head * HEAD
        d_key = dk[...] * cosine[...] - turn(dk[...]) * sine[...]
        out[:, width + at : width + at + HEAD] = d_key.astype(BF16)
        out[:, 2 * width + at : 2 * width + at + HEAD] = dv[...].astype(BF16)


def attend_back(q3, k3, v3, grad, lse, cosine, sine, scalars, local, own, devices, heads):
    count = own * devices
    vmem = pl.BlockSpec(memory_space=pltpu.VMEM)
    return pl.pallas_call(
        functools.partial(attend_back_kernel, local=local, own=own, devices=devices, heads=heads),
        out_shape=jax.ShapeDtypeStruct((count, 3 * heads * HEAD), BF16),
        in_specs=[pl.BlockSpec(memory_space=pltpu.SMEM)] + [vmem] * 7,
        out_specs=vmem,
        scratch_shapes=[pltpu.VMEM((count, HEAD), F32), pltpu.VMEM((count, HEAD), F32)],
        name="attend_back",
    )(scalars, q3, k3, v3, grad, lse, cosine, sine)


def forward_layer(resid, weights, gains, local, tables, scalars):
    w_qkv, w_out, w_in, w_down = weights
    own = resid.shape[0]
    devices = lax.axis_size("tensor")
    heads = w_out.shape[1] // HEAD
    rows_one = gather_rows(layer_norm(resid, gains[0]).astype(BF16))
    qkv = jnp.dot(rows_one, w_qkv, preferred_element_type=F32)
    q3, k3, v3, attended, lse = attend(qkv, *tables, scalars, local, own, devices, heads)
    branch = lax.dot_general(attended, w_out, NT, preferred_element_type=F32)
    mixed = resid + scatter_rows(branch.astype(BF16))
    rows_two = gather_rows(layer_norm(mixed, gains[1]).astype(BF16))
    both = jnp.dot(rows_two, w_in, preferred_element_type=F32)
    units = w_down.shape[1]
    hidden = geglu(both[:, :units], both[:, units:]).astype(BF16)
    down = lax.dot_general(hidden, w_down, NT, preferred_element_type=F32)
    result = mixed + scatter_rows(down.astype(BF16))
    return result, (rows_one, q3, k3, v3, lse, attended, mixed, rows_two, both, hidden)


def backward_layer(grad_out, resid, kept, weights, gains, local, tables, scalars):
    w_qkv, w_out, w_in, w_down = weights
    rows_one, q3, k3, v3, lse, attended, mixed, rows_two, both, hidden = kept
    own = resid.shape[0]
    devices = lax.axis_size("tensor")
    heads = w_out.shape[1] // HEAD
    units = w_down.shape[1]
    outer = functools.partial(jnp.einsum, "sd,sf->df", preferred_element_type=F32)
    grad_rows = gather_rows(grad_out.astype(BF16))
    d_hidden = jnp.dot(grad_rows, w_down, preferred_element_type=F32)
    _, pull_geglu = jax.vjp(geglu, both[:, :units], both[:, units:])
    d_both = jnp.concatenate([part.astype(BF16) for part in pull_geglu(d_hidden)], axis=1)
    d_two = lax.dot_general(d_both, w_in, NT, preferred_element_type=F32)
    d_two = scatter_rows(d_two.astype(BF16))
    grad_mlp = jnp.concatenate(
        [outer(rows_two, d_both).astype(BF16), outer(grad_rows, hidden).astype(BF16)], axis=1
    )
    _, pull_second = jax.vjp(layer_norm, mixed, gains[1])
    d_mixed, gain_two = pull_second(d_two)
    d_mixed = d_mixed + grad_out
    mixed_rows = gather_rows(d_mixed.astype(BF16))
    d_attended = jnp.dot(mixed_rows, w_out, preferred_element_type=F32).astype(BF16)
    d_qkv = attend_back(
        q3, k3, v3, d_attended, lse, *tables, scalars, local, own, devices, heads
    )
    d_one = lax.dot_general(d_qkv, w_qkv, NT, preferred_element_type=F32)
    d_one = scatter_rows(d_one.astype(BF16))
    grad_attn = jnp.concatenate(
        [outer(rows_one, d_qkv).astype(BF16), outer(mixed_rows, attended).astype(BF16)], axis=1
    )
    _, pull_first = jax.vjp(layer_norm, resid, gains[0])
    d_resid, gain_one = pull_first(d_one)
    return d_resid + d_mixed, grad_attn, grad_mlp, jnp.stack([gain_one, gain_two])


def reduce_pack(pack):
    half = pack.shape[1] // 2
    halves = jnp.concatenate([pack[:, :half], pack[:, half:]], axis=0)
    return lax.psum_scatter(halves, ("section", "dp"), scatter_dimension=0, tiled=True)


def local_program(
    inputs, lengths, cotangent, w_query, w_key, w_value, w_out, w_gate, w_up, w_down, norm_gains
):
    section = lax.axis_index("section")
    first = section == 0
    devices = lax.axis_size("tensor")
    own = inputs.shape[1]
    features = inputs.shape[2]
    head_width = w_query.shape[2]
    units = w_gate.shape[2]
    swap = functools.partial(lax.ppermute, axis_name="section", perm=[(0, 1), (1, 0)])

    attn_pack = jnp.concatenate([w_query, w_key, w_value, w_out, norm_gains], axis=2)[0]
    mlp_pack = jnp.concatenate([w_gate, w_up, w_down], axis=2)[0]
    attn_all = lax.all_gather(attn_pack, ("section", "dp"), axis=0, tiled=True)
    mlp_all = lax.all_gather(mlp_pack, ("section", "dp"), axis=0, tiled=True)
    weights = []
    gains = []
    for layer in range(2):
        attn = attn_all[layer * features : (layer + 1) * features]
        mlp = mlp_all[layer * features : (layer + 1) * features]
        weights.append(
            (
                attn[:, : 3 * head_width],
                attn[:, 3 * head_width : 4 * head_width],
                mlp[:, : 2 * units],
                mlp[:, 2 * units :],
            )
        )
        gains.append(attn[:, 4 * head_width :].astype(F32).T)

    position = positions(own, devices)
    tables = [rotary_tables(position, theta) for theta in THETAS]
    length = lax.dynamic_index_in_dim(lengths, section, 0, keepdims=False)[0]
    scalars = jnp.stack([lax.axis_index("tensor").astype(jnp.int32), length.astype(jnp.int32)])

    resid = lax.dynamic_index_in_dim(inputs, section, 0, keepdims=False).astype(F32)
    residuals = []
    kept = []
    produced = []
    for layer in range(2):
        residuals.append(resid)
        result, saved = forward_layer(
            resid, weights[layer], gains[layer], layer == 0, tables[layer], scalars
        )
        kept.append(saved)
        produced.append(result.astype(BF16))
        resid = produced[-1].astype(F32)

    grad = lax.dynamic_index_in_dim(cotangent, section, 0, keepdims=False).astype(F32)
    sent_back = [None, None]
    attn_pieces = [None, None]
    mlp_pieces = [None, None]
    gain_grads = [None, None]
    for layer in (1, 0):
        d_resid, grad_attn, grad_mlp, gain_grads[layer] = backward_layer(
            grad,
            residuals[layer],
            kept[layer],
            weights[layer],
            gains[layer],
            layer == 0,
            tables[layer],
            scalars,
        )
        mlp_pieces[layer] = reduce_pack(grad_mlp)
        attn_pieces[layer] = reduce_pack(grad_attn)
        sent_back[layer] = d_resid.astype(BF16)
        grad = sent_back[layer].astype(F32)

    def by_layer(pair):
        mine = jnp.where(first, pair[0], pair[1])
        other = swap(jnp.where(first, pair[1], pair[0]))
        return jnp.stack([jnp.where(first, mine, other), jnp.where(first, other, mine)])[None]

    def whole(pair):
        mine = jnp.where(first, pair[0], pair[1])
        other = swap(jnp.where(first, pair[1], pair[0]))
        low = jnp.where(first, mine, other)
        high = jnp.where(first, other, mine)
        return jnp.concatenate([low, high], axis=1).astype(F32)[None]

    attn_grad = whole(attn_pieces)
    mlp_grad = whole(mlp_pieces)
    summed = lax.psum(jnp.concatenate(gain_grads, axis=0), ("section", "dp", "tensor"))
    shard = norm_gains.shape[1]
    gain_grad = lax.dynamic_slice(
        summed, (2 * section, lax.axis_index("dp") * shard), (2, shard)
    ).T[None]
    return (
        by_layer(produced),
        by_layer(sent_back),
        attn_grad[:, :, :head_width],
        attn_grad[:, :, head_width : 2 * head_width],
        attn_grad[:, :, 2 * head_width : 3 * head_width],
        attn_grad[:, :, 3 * head_width :],
        mlp_grad[:, :, :units],
        mlp_grad[:, :, units : 2 * units],
        mlp_grad[:, :, 2 * units :],
        gain_grad,
    )


def solution(mesh):
    rows = P(None, ("dp", "tensor"), None)
    weight = P("section", "dp", "tensor")
    gain = P("section", "dp", None)
    out_rows = P("section", None, ("dp", "tensor"), None)
    return jax.shard_map(
        local_program,
        mesh=mesh,
        in_specs=(rows, P(None, "dp"), rows) + (weight,) * 7 + (gain,),
        out_specs=(out_rows, out_rows) + (weight,) * 7 + (gain,),
        check_vma=False,
    )
```

```python
import functools

import jax
import jax.numpy as jnp
from jax import lax
from jax.experimental import pallas as pl
from jax.experimental.pallas import tpu as pltpu
from jax.sharding import PartitionSpec as P

HEAD = 64
HALF_WINDOW = 64
THETAS = (10000.0, 160000.0)
EPSILON = 1e-05
SCALE = HEAD ** (-0.5)
MASKED = -1e30
BF16 = jnp.bfloat16
F32 = jnp.float32
NT = (((1,), (1,)), ((), ()))


def layer_norm(rows, gain):
    centre = rows - jnp.mean(rows, axis=-1, keepdims=True)
    variance = jnp.mean(centre * centre, axis=-1, keepdims=True)
    return centre * lax.rsqrt(variance + EPSILON) * gain


def geglu(gate, upper):
    return jax.nn.gelu(gate, approximate=False) * upper


def exchange(value, by):
    count = lax.axis_size("tensor")
    return lax.ppermute(value, "tensor", [(i, i ^ by) for i in range(count)])


def gather_rows(rows):
    return [rows] + [exchange(rows, by) for by in range(1, lax.axis_size("tensor"))]


def scatter_rows(blocks):
    moved = [exchange(block, by) for by, block in enumerate(blocks) if by]
    total = blocks[0].astype(F32)
    for block in moved:
        total = total + block.astype(F32)
    return total


def over(value, axis, by):
    count = lax.axis_size(axis)
    return lax.ppermute(value, axis, [(i, i ^ by) for i in range(count)])


def butterfly(value, axes):
    for axis in axes:
        by = 1
        while by < lax.axis_size(axis):
            value = value + over(value, axis, by)
            by *= 2
    return value


def dp_gather(shard):
    count = lax.axis_size("dp")
    if count > 8:
        return lax.all_gather(shard, "dp", axis=0, tiled=True)
    rows = shard.shape[0]
    index = lax.axis_index("dp")
    full = jnp.zeros((count * rows,) + shard.shape[1:], shard.dtype)
    for by in range(count):
        block = over(shard, "dp", by) if by else shard
        full = lax.dynamic_update_slice_in_dim(full, block, (index ^ by) * rows, 0)
    return full


def dp_scatter(full):
    count = lax.axis_size("dp")
    if count > 8:
        return lax.psum_scatter(full, "dp", scatter_dimension=0, tiled=True)
    rows = full.shape[0] // count
    index = lax.axis_index("dp")
    total = None
    for by in range(count):
        block = lax.dynamic_slice_in_dim(full, (index ^ by) * rows, rows, 0)
        block = (over(block, "dp", by) if by else block).astype(F32)
        total = block if total is None else total + block
    return total.astype(full.dtype)


def swap(value):
    return over(value, "section", 1)


def positions(own, devices):
    index = lax.axis_index("tensor")
    row = jnp.arange(own * devices, dtype=jnp.int32)
    return ((row // own) ^ index) * own + row % own


def rotary_tables(position, theta):
    index = jnp.arange(HEAD // 2, dtype=F32)[None, :]
    inverse = jnp.exp(-jnp.log(F32(theta)) * (2.0 * index / HEAD))
    angle = position.astype(F32)[:, None] * inverse
    cosine = jnp.cos(angle)
    sine = jnp.sin(angle)
    return (
        jnp.concatenate([cosine, cosine], axis=1),
        jnp.concatenate([sine, sine], axis=1),
    )


def turn(rows):
    half = HEAD // 2
    return jnp.concatenate([-rows[:, half:], rows[:, :half]], axis=1)


def neighbours(scalars, block, own, devices):
    index = scalars[0]
    place = index ^ block
    before = (jnp.maximum(place - 1, 0) ^ index) * own + own - HALF_WINDOW
    after = (jnp.minimum(place + 1, devices - 1) ^ index) * own
    return place, pl.multiple_of(before, HALF_WINDOW), pl.multiple_of(after, HALF_WINDOW)


def attend_kernel(scalars, cosine, sine, *refs, local, own, devices, heads):
    blocks = refs[:devices]
    q3, k3, v3, out, lse = refs[devices:]
    count = own * devices
    width = heads * HEAD
    length = scalars[1]
    for head in range(heads):
        at = head * HEAD
        for index, qkv in enumerate(blocks):
            here = slice(index * own, (index + 1) * own)
            for part, store in ((0, q3), (1, k3)):
                rows = qkv[:, part * width + at : part * width + at + HEAD]
                turned = rows * cosine[here, :] + turn(rows) * sine[here, :]
                store[head, here, :] = turned.astype(BF16)
            v3[head, here, :] = qkv[:, 2 * width + at : 2 * width + at + HEAD].astype(BF16)
    for head in range(heads):

        def step(block, carry):
            start = pl.multiple_of(block * own, own)
            query = q3[head, pl.ds(start, own), :]
            if local:
                place, before, after = neighbours(scalars, block, own, devices)
                key = jnp.concatenate(
                    [
                        k3[head, pl.ds(before, HALF_WINDOW), :],
                        k3[head, pl.ds(start, own), :],
                        k3[head, pl.ds(after, HALF_WINDOW), :],
                    ],
                    axis=0,
                )
                value = jnp.concatenate(
                    [
                        v3[head, pl.ds(before, HALF_WINDOW), :],
                        v3[head, pl.ds(start, own), :],
                        v3[head, pl.ds(after, HALF_WINDOW), :],
                    ],
                    axis=0,
                )
                span = own + 2 * HALF_WINDOW
                shape = (own, span)
                row = lax.broadcasted_iota(jnp.int32, shape, 0)
                column = lax.broadcasted_iota(jnp.int32, shape, 1) - HALF_WINDOW
                spot = column + place * own
                near = jnp.abs(row - column) <= HALF_WINDOW
                allowed = (near & (spot >= 0) & (spot < length)) | (row == column)
            else:
                key = k3[head]
                value = v3[head]
                shape = (own, count)
                row = lax.broadcasted_iota(jnp.int32, shape, 0) + start
                column = lax.broadcasted_iota(jnp.int32, shape, 1)
                spot = ((column // own) ^ scalars[0]) * own + column % own
                allowed = (spot < length) | (row == column)
            raw = lax.dot_general(query, key, NT, preferred_element_type=F32) * SCALE
            scores = jnp.where(allowed, raw, MASKED)
            highest = jnp.max(scores, axis=1, keepdims=True)
            lifted = jnp.exp(scores - highest)
            summed = jnp.sum(lifted, axis=1, keepdims=True)
            probs = (lifted / summed).astype(BF16)
            got = jnp.dot(probs, value, preferred_element_type=F32)
            out[pl.ds(start, own), head * HEAD : (head + 1) * HEAD] = got.astype(BF16)
            total = jnp.broadcast_to(highest + jnp.log(summed), (own, 128))
            lse[head, :, pl.ds(start, own)] = total.T[:8]
            return carry

        lax.fori_loop(0, devices, step, 0)


def attend(qkv, cosine, sine, scalars, local, own, devices, heads):
    count = own * devices
    split = jax.ShapeDtypeStruct((heads, count, HEAD), BF16)
    vmem = pl.BlockSpec(memory_space=pltpu.VMEM)
    return pl.pallas_call(
        functools.partial(attend_kernel, local=local, own=own, devices=devices, heads=heads),
        out_shape=(
            split,
            split,
            split,
            jax.ShapeDtypeStruct((count, heads * HEAD), BF16),
            jax.ShapeDtypeStruct((heads, 8, count), F32),
        ),
        in_specs=[pl.BlockSpec(memory_space=pltpu.SMEM)] + [vmem] * (2 + devices),
        out_specs=(vmem, vmem, vmem, vmem, vmem),
        name="attend",
    )(scalars, cosine, sine, *qkv)


def attend_back_kernel(
    scalars, q3, k3, v3, lse, cosine, sine, *refs, local, own, devices, heads
):
    blocks = refs[:devices]
    out, dk, dv, grad = refs[devices:]
    for index, block in enumerate(blocks):
        grad[index * own : (index + 1) * own, :] = block[...]
    count = own * devices
    width = heads * HEAD
    length = scalars[1]
    for head in range(heads):
        dk[...] = jnp.zeros_like(dk)
        dv[...] = jnp.zeros_like(dv)

        def step(block, carry):
            start = pl.multiple_of(block * own, own)
            here = pl.ds(start, own)
            query = q3[head, here, :]
            upstream = grad[here, head * HEAD : (head + 1) * HEAD]
            if local:
                place, before, after = neighbours(scalars, block, own, devices)
                pieces = (
                    (pl.ds(before, HALF_WINDOW), 0, HALF_WINDOW),
                    (here, HALF_WINDOW, HALF_WINDOW + own),
                    (pl.ds(after, HALF_WINDOW), HALF_WINDOW + own, 2 * HALF_WINDOW + own),
                )
                key = jnp.concatenate([k3[head, piece, :] for piece, _, _ in pieces], axis=0)
                value = jnp.concatenate([v3[head, piece, :] for piece, _, _ in pieces], axis=0)
                shape = (own + 2 * HALF_WINDOW, own)
                row = lax.broadcasted_iota(jnp.int32, shape, 1)
                column = lax.broadcasted_iota(jnp.int32, shape, 0) - HALF_WINDOW
                spot = column + place * own
                near = jnp.abs(row - column) <= HALF_WINDOW
                allowed = (near & (spot >= 0) & (spot < length)) | (row == column)
            else:
                pieces = ((slice(None), 0, count),)
                key = k3[head]
                value = v3[head]
                shape = (count, own)
                row = lax.broadcasted_iota(jnp.int32, shape, 1) + start
                column = lax.broadcasted_iota(jnp.int32, shape, 0)
                spot = ((column // own) ^ scalars[0]) * own + column % own
                allowed = (spot < length) | (row == column)
            raw = lax.dot_general(key, query, NT, preferred_element_type=F32) * SCALE
            scores = jnp.where(allowed, raw, MASKED)
            probs = jnp.exp(scores - lse[head, 0:1, here])
            d_probs = lax.dot_general(value, upstream, NT, preferred_element_type=F32)
            weighted = jnp.sum(probs * d_probs, axis=0, keepdims=True)
            d_scores = (probs * (d_probs - weighted)).astype(BF16)
            d_key = jnp.dot(d_scores, query, preferred_element_type=F32) * SCALE
            d_value = jnp.dot(probs.astype(BF16), upstream, preferred_element_type=F32)
            for piece, low, high in pieces:
                dk[piece, :] += d_key[low:high]
                dv[piece, :] += d_value[low:high]
            d_query = jnp.dot(key.T, d_scores, preferred_element_type=F32).T * SCALE
            d_query = d_query * cosine[here, :] - turn(d_query) * sine[here, :]
            out[here, head * HEAD : (head + 1) * HEAD] = d_query.astype(BF16)
            return carry

        lax.fori_loop(0, devices, step, 0)
        at = head * HEAD
        d_key = dk[...] * cosine[...] - turn(dk[...]) * sine[...]
        out[:, width + at : width + at + HEAD] = d_key.astype(BF16)
        out[:, 2 * width + at : 2 * width + at + HEAD] = dv[...].astype(BF16)


def attend_back(q3, k3, v3, grad, lse, cosine, sine, scalars, local, own, devices, heads):
    count = own * devices
    vmem = pl.BlockSpec(memory_space=pltpu.VMEM)
    return pl.pallas_call(
        functools.partial(attend_back_kernel, local=local, own=own, devices=devices, heads=heads),
        out_shape=jax.ShapeDtypeStruct((count, 3 * heads * HEAD), BF16),
        in_specs=[pl.BlockSpec(memory_space=pltpu.SMEM)] + [vmem] * (6 + devices),
        out_specs=vmem,
        scratch_shapes=[
            pltpu.VMEM((count, HEAD), F32),
            pltpu.VMEM((count, HEAD), F32),
            pltpu.VMEM((count, heads * HEAD), BF16),
        ],
        name="attend_back",
    )(scalars, q3, k3, v3, lse, cosine, sine, *grad)


def cut(rows, own):
    return [rows[at : at + own] for at in range(0, rows.shape[0], own)]


def product(blocks, weight):
    return [jnp.dot(block, weight, preferred_element_type=F32) for block in blocks]


def product_back(blocks, weight):
    return [lax.dot_general(block, weight, NT, preferred_element_type=F32) for block in blocks]


def low(blocks):
    return [block.astype(BF16) for block in blocks]


def forward_layer(resid, weights, gains, local, tables, scalars):
    w_qkv, w_out, w_in, w_down = weights
    own = resid.shape[0]
    devices = lax.axis_size("tensor")
    heads = w_out().shape[1] // HEAD
    rows_one = gather_rows(layer_norm(resid, gains[0]).astype(BF16))
    qkv = product(rows_one, w_qkv())
    q3, k3, v3, attended, lse = attend(qkv, *tables, scalars, local, own, devices, heads)
    branch = low(product_back(cut(attended, own), w_out()))
    mixed = resid + scatter_rows(branch)
    rows_two = gather_rows(layer_norm(mixed, gains[1]).astype(BF16))
    both = product(rows_two, w_in())
    units = w_down().shape[1]
    hidden = [geglu(block[:, :units], block[:, units:]).astype(BF16) for block in both]
    result = mixed + scatter_rows(low(product_back(hidden, w_down())))
    return result, (rows_one, q3, k3, v3, lse, attended, mixed, rows_two, both, hidden)


def backward_layer(grad_out, resid, kept, weights, gains, local, tables, scalars):
    w_qkv, w_out, w_in, w_down = [weight() for weight in weights]
    rows_one, q3, k3, v3, lse, attended, mixed, rows_two, both, hidden = kept
    own = resid.shape[0]
    devices = lax.axis_size("tensor")
    heads = w_out.shape[1] // HEAD
    units = w_down.shape[1]

    def outer(left, right):
        left, right = [
            jnp.concatenate(side, axis=0) if isinstance(side, list) else side
            for side in (left, right)
        ]
        return jnp.einsum("sd,sf->df", left, right, preferred_element_type=F32).astype(BF16)

    grad_rows = gather_rows(grad_out.astype(BF16))
    d_both = []
    for block, d_hidden in zip(both, product(grad_rows, w_down)):
        _, pull_geglu = jax.vjp(geglu, block[:, :units], block[:, units:])
        d_both.append(jnp.concatenate(low(pull_geglu(d_hidden)), axis=1))
    d_two = scatter_rows(low(product_back(d_both, w_in)))
    grad_mlp = jnp.concatenate([outer(rows_two, d_both), outer(grad_rows, hidden)], axis=1)
    _, pull_second = jax.vjp(layer_norm, mixed, gains[1])
    d_mixed, gain_two = pull_second(d_two)
    d_mixed = d_mixed + grad_out
    mixed_rows = gather_rows(d_mixed.astype(BF16))
    d_attended = low(product(mixed_rows, w_out))
    d_qkv = attend_back(
        q3, k3, v3, d_attended, lse, *tables, scalars, local, own, devices, heads
    )
    d_one = scatter_rows(low(product_back(cut(d_qkv, own), w_qkv)))
    grad_attn = jnp.concatenate([outer(rows_one, d_qkv), outer(mixed_rows, attended)], axis=1)
    _, pull_first = jax.vjp(layer_norm, resid, gains[0])
    d_resid, gain_one = pull_first(d_one)
    return d_resid + d_mixed, grad_attn, grad_mlp, jnp.stack([gain_one, gain_two])


def reduce_pack(pack):
    half = pack.shape[1] // 2
    halves = jnp.concatenate([pack[:, :half], pack[:, half:]], axis=0)
    return lax.psum_scatter(halves, ("section", "dp"), scatter_dimension=0, tiled=True)


def reduce_last(pack):
    half = pack.shape[1] // 2
    first = lax.axis_index("section") == 0
    mine = jnp.where(first, pack[:, :half], pack[:, half:])
    other = swap(jnp.where(first, pack[:, half:], pack[:, :half]))
    return dp_scatter((mine.astype(F32) + other.astype(F32)).astype(BF16))


def local_program(
    inputs, lengths, cotangent, w_query, w_key, w_value, w_out, w_gate, w_up, w_down, norm_gains
):
    section = lax.axis_index("section")
    first = section == 0
    devices = lax.axis_size("tensor")
    own = inputs.shape[1]
    features = inputs.shape[2]
    head_width = w_query.shape[2]
    units = w_gate.shape[2]

    shard = norm_gains.shape[1]
    spread = lax.dynamic_update_slice(
        jnp.zeros((4, features), F32),
        norm_gains[0].astype(F32).T,
        (2 * section, lax.axis_index("dp") * shard),
    )
    all_gains = butterfly(spread, ("section", "dp"))
    gains = [all_gains[:2], all_gains[2:]]

    attn_shard = jnp.concatenate([w_query, w_key, w_value, w_out], axis=2)[0]
    half = 2 * head_width
    own_half = jnp.where(first, attn_shard[:, :half], attn_shard[:, half:])
    got_half = swap(jnp.where(first, attn_shard[:, half:], attn_shard[:, :half]))
    mine = dp_gather(jnp.where(first, own_half, got_half))
    other = swap(mine)
    low_half = jnp.where(first, mine, other)
    high_half = jnp.where(first, other, mine)

    mlp_pack = jnp.concatenate([w_gate, w_up, w_down], axis=2)[0]
    second, mlp_pack, _ = lax.optimization_barrier(
        (jnp.where(first, got_half, own_half), mlp_pack, other)
    )
    mlp_all = lax.all_gather(mlp_pack, ("section", "dp"), axis=0, tiled=True)
    second = lax.all_gather(second, ("section", "dp"), axis=0, tiled=True)
    halves = [(low_half, high_half), (second[:features], second[features:])]
    weights = []
    for layer in range(2):
        low_part, high_part = halves[layer]
        mlp = mlp_all[layer * features : (layer + 1) * features]
        qkv = jnp.concatenate([low_part, high_part[:, :head_width]], axis=1)
        weights.append(
            (
                lambda qkv=qkv: qkv,
                lambda high_part=high_part: high_part[:, head_width:],
                lambda mlp=mlp: mlp[:, : 2 * units],
                lambda mlp=mlp: mlp[:, 2 * units :],
            )
        )

    position = positions(own, devices)
    tables = [rotary_tables(position, theta) for theta in THETAS]
    length = lax.dynamic_index_in_dim(lengths, section, 0, keepdims=False)[0]
    scalars = jnp.stack([lax.axis_index("tensor").astype(jnp.int32), length.astype(jnp.int32)])

    resid = lax.dynamic_index_in_dim(inputs, section, 0, keepdims=False).astype(F32)
    residuals = []
    kept = []
    produced = []
    for layer in range(2):
        residuals.append(resid)
        result, saved = forward_layer(
            resid, weights[layer], gains[layer], layer == 0, tables[layer], scalars
        )
        kept.append(saved)
        produced.append(result.astype(BF16))
        resid = produced[-1].astype(F32)

    grad = lax.dynamic_index_in_dim(cotangent, section, 0, keepdims=False).astype(F32)
    sent_back = [None, None]
    attn_pieces = [None, None]
    mlp_pieces = [None, None]
    gain_grads = [None, None]
    for layer in (1, 0):
        d_resid, grad_attn, grad_mlp, gain_grads[layer] = backward_layer(
            grad,
            residuals[layer],
            kept[layer],
            weights[layer],
            gains[layer],
            layer == 0,
            tables[layer],
            scalars,
        )
        mlp_pieces[layer] = reduce_pack(grad_mlp)
        attn_pieces[layer] = reduce_pack(grad_attn) if layer else reduce_last(grad_attn)
        sent_back[layer] = d_resid.astype(BF16)
        grad = sent_back[layer].astype(F32)

    def by_layer(pair):
        mine = jnp.where(first, pair[0], pair[1])
        other = swap(jnp.where(first, pair[1], pair[0]))
        return jnp.stack([jnp.where(first, mine, other), jnp.where(first, other, mine)])[None]

    def whole(pair):
        mine = jnp.where(first, pair[0], pair[1])
        other = swap(jnp.where(first, pair[1], pair[0]))
        low = jnp.where(first, mine, other)
        high = jnp.where(first, other, mine)
        return jnp.concatenate([low, high], axis=1).astype(F32)[None]

    attn_grad = whole(attn_pieces)
    mlp_grad = whole(mlp_pieces)
    summed = butterfly(jnp.concatenate(gain_grads, axis=0), ("tensor", "section", "dp"))
    gain_grad = lax.dynamic_slice(
        summed, (2 * section, lax.axis_index("dp") * shard), (2, shard)
    ).T[None]
    return (
        by_layer(produced),
        by_layer(sent_back),
        attn_grad[:, :, :head_width],
        attn_grad[:, :, head_width : 2 * head_width],
        attn_grad[:, :, 2 * head_width : 3 * head_width],
        attn_grad[:, :, 3 * head_width :],
        mlp_grad[:, :, :units],
        mlp_grad[:, :, units : 2 * units],
        mlp_grad[:, :, 2 * units :],
        gain_grad,
    )


def solution(mesh):
    rows = P(None, ("dp", "tensor"), None)
    weight = P("section", "dp", "tensor")
    gain = P("section", "dp", None)
    out_rows = P("section", None, ("dp", "tensor"), None)
    return jax.shard_map(
        local_program,
        mesh=mesh,
        in_specs=(rows, P(None, "dp"), rows) + (weight,) * 7 + (gain,),
        out_specs=(out_rows, out_rows) + (weight,) * 7 + (gain,),
        check_vma=False,
    )
```

```python
import functools

import jax
import jax.numpy as jnp
from jax import lax
from jax.experimental import pallas as pl
from jax.experimental.pallas import tpu as pltpu
from jax.sharding import PartitionSpec as P

HEAD = 64
HALF_WINDOW = 64
THETAS = (10000.0, 160000.0)
EPSILON = 1e-05
SCALE = HEAD ** (-0.5)
MASKED = -1e30
BF16 = jnp.bfloat16
F32 = jnp.float32
NT = (((1,), (1,)), ((), ()))


def layer_norm(rows, gain):
    centre = rows - jnp.mean(rows, axis=-1, keepdims=True)
    variance = jnp.mean(centre * centre, axis=-1, keepdims=True)
    return centre * lax.rsqrt(variance + EPSILON) * gain


def geglu(gate, upper):
    return jax.nn.gelu(gate, approximate=False) * upper


def exchange(value, by):
    count = lax.axis_size("tensor")
    return lax.ppermute(value, "tensor", [(i, i ^ by) for i in range(count)])


def gather_rows(rows):
    count = lax.axis_size("tensor")
    return jnp.concatenate([rows] + [exchange(rows, by) for by in range(1, count)], axis=0)


def scatter_rows(partial):
    count = lax.axis_size("tensor")
    own = partial.shape[0] // count
    total = partial[:own].astype(F32)
    for by in range(1, count):
        total = total + exchange(partial[by * own : (by + 1) * own], by).astype(F32)
    return total


def butterfly(value, axes):
    for axis in axes:
        count = lax.axis_size(axis)
        by = 1
        while by < count:
            value = value + lax.ppermute(value, axis, [(i, i ^ by) for i in range(count)])
            by *= 2
    return value


def positions(own, devices):
    index = lax.axis_index("tensor")
    row = jnp.arange(own * devices, dtype=jnp.int32)
    return ((row // own) ^ index) * own + row % own


def rotary_tables(position, theta):
    index = jnp.arange(HEAD // 2, dtype=F32)[None, :]
    inverse = jnp.exp(-jnp.log(F32(theta)) * (2.0 * index / HEAD))
    angle = position.astype(F32)[:, None] * inverse
    cosine = jnp.cos(angle)
    sine = jnp.sin(angle)
    return (
        jnp.concatenate([cosine, cosine], axis=1),
        jnp.concatenate([sine, sine], axis=1),
    )


def turn(rows):
    half = HEAD // 2
    return jnp.concatenate([-rows[:, half:], rows[:, :half]], axis=1)


def neighbours(scalars, block, own, devices):
    index = scalars[0]
    place = index ^ block
    before = (jnp.maximum(place - 1, 0) ^ index) * own + own - HALF_WINDOW
    after = (jnp.minimum(place + 1, devices - 1) ^ index) * own
    return place, pl.multiple_of(before, HALF_WINDOW), pl.multiple_of(after, HALF_WINDOW)


def attend_kernel(scalars, qkv, cosine, sine, q3, k3, v3, out, lse, o3, *, local, own, devices, heads):
    count = own * devices
    width = heads * HEAD
    length = scalars[1]
    for head in range(heads):
        at = head * HEAD
        for part, store in ((0, q3), (1, k3)):
            rows = qkv[:, part * width + at : part * width + at + HEAD]
            store[head] = (rows * cosine[...] + turn(rows) * sine[...]).astype(BF16)
        v3[head] = qkv[:, 2 * width + at : 2 * width + at + HEAD].astype(BF16)
    def step(at, carry):
        head = at // devices
        block = at % devices
        start = pl.multiple_of(block * own, own)
        query = q3[head, pl.ds(start, own), :]
        if local:
            place, before, after = neighbours(scalars, block, own, devices)
            key = jnp.concatenate(
                [
                    k3[head, pl.ds(before, HALF_WINDOW), :],
                    k3[head, pl.ds(start, own), :],
                    k3[head, pl.ds(after, HALF_WINDOW), :],
                ],
                axis=0,
            )
            value = jnp.concatenate(
                [
                    v3[head, pl.ds(before, HALF_WINDOW), :],
                    v3[head, pl.ds(start, own), :],
                    v3[head, pl.ds(after, HALF_WINDOW), :],
                ],
                axis=0,
            )
            span = own + 2 * HALF_WINDOW
            shape = (own, span)
            row = lax.broadcasted_iota(jnp.int32, shape, 0)
            column = lax.broadcasted_iota(jnp.int32, shape, 1) - HALF_WINDOW
            spot = column + place * own
            near = jnp.abs(row - column) <= HALF_WINDOW
            allowed = (near & (spot >= 0) & (spot < length)) | (row == column)
        else:
            key = k3[head]
            value = v3[head]
            shape = (own, count)
            row = lax.broadcasted_iota(jnp.int32, shape, 0) + start
            column = lax.broadcasted_iota(jnp.int32, shape, 1)
            spot = ((column // own) ^ scalars[0]) * own + column % own
            allowed = (spot < length) | (row == column)
        raw = lax.dot_general(query, key, NT, preferred_element_type=F32) * SCALE
        scores = jnp.where(allowed, raw, MASKED)
        highest = jnp.max(scores, axis=1, keepdims=True)
        lifted = jnp.exp(scores - highest)
        summed = jnp.sum(lifted, axis=1, keepdims=True)
        probs = (lifted / summed).astype(BF16)
        got = jnp.dot(probs, value, preferred_element_type=F32)
        o3[head, pl.ds(start, own), :] = got.astype(BF16)
        total = jnp.broadcast_to(highest + jnp.log(summed), (own, 128))
        lse[head, :, pl.ds(start, own)] = total.T[:8]
        return carry

    lax.fori_loop(0, heads * devices, step, 0)
    for head in range(heads):
        out[:, head * HEAD : (head + 1) * HEAD] = o3[head]


def attend(qkv, cosine, sine, scalars, local, own, devices, heads):
    count = own * devices
    split = jax.ShapeDtypeStruct((heads, count, HEAD), BF16)
    vmem = pl.BlockSpec(memory_space=pltpu.VMEM)
    return pl.pallas_call(
        functools.partial(attend_kernel, local=local, own=own, devices=devices, heads=heads),
        out_shape=(
            split,
            split,
            split,
            jax.ShapeDtypeStruct((count, heads * HEAD), BF16),
            jax.ShapeDtypeStruct((heads, 8, count), F32),
        ),
        in_specs=[pl.BlockSpec(memory_space=pltpu.SMEM), vmem, vmem, vmem],
        out_specs=(vmem, vmem, vmem, vmem, vmem),
        scratch_shapes=[pltpu.VMEM((heads, count, HEAD), BF16)],
        name="attend",
    )(scalars, qkv, cosine, sine)


def attend_back_kernel(
    scalars, q3, k3, v3, grad, lse, cosine, sine, out, dq, dk, dv, grad3, *, local, own, devices, heads
):
    count = own * devices
    width = heads * HEAD
    length = scalars[1]
    dk[...] = jnp.zeros_like(dk)
    dv[...] = jnp.zeros_like(dv)
    for head in range(heads):
        grad3[head] = grad[:, head * HEAD : (head + 1) * HEAD]

    def step(at, carry):
        head = at // devices
        block = at % devices
        start = pl.multiple_of(block * own, own)
        here = pl.ds(start, own)
        query = q3[head, here, :]
        upstream = grad3[head, here, :]
        if local:
            place, before, after = neighbours(scalars, block, own, devices)
            pieces = (
                (pl.ds(before, HALF_WINDOW), 0, HALF_WINDOW),
                (here, HALF_WINDOW, HALF_WINDOW + own),
                (pl.ds(after, HALF_WINDOW), HALF_WINDOW + own, 2 * HALF_WINDOW + own),
            )
            key = jnp.concatenate([k3[head, piece, :] for piece, _, _ in pieces], axis=0)
            value = jnp.concatenate([v3[head, piece, :] for piece, _, _ in pieces], axis=0)
            shape = (own + 2 * HALF_WINDOW, own)
            row = lax.broadcasted_iota(jnp.int32, shape, 1)
            column = lax.broadcasted_iota(jnp.int32, shape, 0) - HALF_WINDOW
            spot = column + place * own
            near = jnp.abs(row - column) <= HALF_WINDOW
            allowed = (near & (spot >= 0) & (spot < length)) | (row == column)
        else:
            pieces = ((slice(None), 0, count),)
            key = k3[head]
            value = v3[head]
            shape = (count, own)
            row = lax.broadcasted_iota(jnp.int32, shape, 1) + start
            column = lax.broadcasted_iota(jnp.int32, shape, 0)
            spot = ((column // own) ^ scalars[0]) * own + column % own
            allowed = (spot < length) | (row == column)
        raw = lax.dot_general(key, query, NT, preferred_element_type=F32) * SCALE
        scores = jnp.where(allowed, raw, MASKED)
        probs = jnp.exp(scores - lse[head, 0:1, here])
        d_probs = lax.dot_general(value, upstream, NT, preferred_element_type=F32)
        weighted = jnp.sum(probs * d_probs, axis=0, keepdims=True)
        d_scores = (probs * (d_probs - weighted)).astype(BF16)
        d_key = jnp.dot(d_scores, query, preferred_element_type=F32) * SCALE
        d_value = jnp.dot(probs.astype(BF16), upstream, preferred_element_type=F32)
        for piece, low, high in pieces:
            dk[head, piece, :] += d_key[low:high]
            dv[head, piece, :] += d_value[low:high]
        d_query = jnp.dot(key.T, d_scores, preferred_element_type=F32).T * SCALE
        d_query = d_query * cosine[here, :] - turn(d_query) * sine[here, :]
        dq[head, here, :] = d_query.astype(BF16)
        return carry

    lax.fori_loop(0, heads * devices, step, 0)
    for head in range(heads):
        at = head * HEAD
        d_key = dk[head] * cosine[...] - turn(dk[head]) * sine[...]
        out[:, at : at + HEAD] = dq[head]
        out[:, width + at : width + at + HEAD] = d_key.astype(BF16)
        out[:, 2 * width + at : 2 * width + at + HEAD] = dv[head].astype(BF16)


def attend_back(q3, k3, v3, grad, lse, cosine, sine, scalars, local, own, devices, heads):
    count = own * devices
    vmem = pl.BlockSpec(memory_space=pltpu.VMEM)
    return pl.pallas_call(
        functools.partial(attend_back_kernel, local=local, own=own, devices=devices, heads=heads),
        out_shape=jax.ShapeDtypeStruct((count, 3 * heads * HEAD), BF16),
        in_specs=[pl.BlockSpec(memory_space=pltpu.SMEM)] + [vmem] * 7,
        out_specs=vmem,
        scratch_shapes=[
            pltpu.VMEM((heads, count, HEAD), BF16),
            pltpu.VMEM((heads, count, HEAD), F32),
            pltpu.VMEM((heads, count, HEAD), F32),
            pltpu.VMEM((heads, count, HEAD), BF16),
        ],
        name="attend_back",
    )(scalars, q3, k3, v3, grad, lse, cosine, sine)


def forward_layer(resid, weights, gains, local, tables, scalars):
    w_qkv, w_out, w_in, w_down = weights
    own = resid.shape[0]
    devices = lax.axis_size("tensor")
    heads = w_out.shape[1] // HEAD
    rows_one = gather_rows(layer_norm(resid, gains[0]).astype(BF16))
    qkv = jnp.dot(rows_one, w_qkv, preferred_element_type=F32)
    q3, k3, v3, attended, lse = attend(qkv, *tables, scalars, local, own, devices, heads)
    branch = lax.dot_general(attended, w_out, NT, preferred_element_type=F32)
    mixed = resid + scatter_rows(branch.astype(BF16))
    rows_two = gather_rows(layer_norm(mixed, gains[1]).astype(BF16))
    both = jnp.dot(rows_two, w_in, preferred_element_type=F32)
    units = w_down.shape[1]
    hidden = geglu(both[:, :units], both[:, units:]).astype(BF16)
    down = lax.dot_general(hidden, w_down, NT, preferred_element_type=F32)
    result = mixed + scatter_rows(down.astype(BF16))
    return result, (rows_one, q3, k3, v3, lse, attended, mixed, rows_two, both, hidden)


def backward_layer(grad_out, resid, kept, weights, gains, local, tables, scalars):
    w_qkv, w_out, w_in, w_down = weights
    rows_one, q3, k3, v3, lse, attended, mixed, rows_two, both, hidden = kept
    own = resid.shape[0]
    devices = lax.axis_size("tensor")
    heads = w_out.shape[1] // HEAD
    units = w_down.shape[1]
    outer = functools.partial(jnp.einsum, "sd,sf->df", preferred_element_type=F32)
    grad_rows = gather_rows(grad_out.astype(BF16))
    d_hidden = jnp.dot(grad_rows, w_down, preferred_element_type=F32)
    _, pull_geglu = jax.vjp(geglu, both[:, :units], both[:, units:])
    d_both = jnp.concatenate([part.astype(BF16) for part in pull_geglu(d_hidden)], axis=1)
    d_two = lax.dot_general(d_both, w_in, NT, preferred_element_type=F32)
    d_two = scatter_rows(d_two.astype(BF16))
    grad_mlp = jnp.concatenate(
        [outer(rows_two, d_both).astype(BF16), outer(grad_rows, hidden).astype(BF16)], axis=1
    )
    _, pull_second = jax.vjp(layer_norm, mixed, gains[1])
    d_mixed, gain_two = pull_second(d_two)
    d_mixed = d_mixed + grad_out
    mixed_rows = gather_rows(d_mixed.astype(BF16))
    d_attended = jnp.dot(mixed_rows, w_out, preferred_element_type=F32).astype(BF16)
    d_qkv = attend_back(
        q3, k3, v3, d_attended, lse, *tables, scalars, local, own, devices, heads
    )
    grad_attn = jnp.concatenate(
        [outer(rows_one, d_qkv).astype(BF16), outer(mixed_rows, attended).astype(BF16)], axis=1
    )
    if local:
        grad_attn, d_qkv = lax.optimization_barrier((grad_attn, d_qkv))
    d_one = lax.dot_general(d_qkv, w_qkv, NT, preferred_element_type=F32)
    d_one = scatter_rows(d_one.astype(BF16))
    _, pull_first = jax.vjp(layer_norm, resid, gains[0])
    d_resid, gain_one = pull_first(d_one)
    return d_resid + d_mixed, grad_attn, grad_mlp, jnp.stack([gain_one, gain_two])


def reduce_pack(pack):
    half = pack.shape[1] // 2
    halves = jnp.concatenate([pack[:, :half], pack[:, half:]], axis=0)
    return lax.psum_scatter(halves, ("section", "dp"), scatter_dimension=0, tiled=True)


def local_program(
    inputs, lengths, cotangent, w_query, w_key, w_value, w_out, w_gate, w_up, w_down, norm_gains
):
    section = lax.axis_index("section")
    first = section == 0
    devices = lax.axis_size("tensor")
    own = inputs.shape[1]
    features = inputs.shape[2]
    head_width = w_query.shape[2]
    units = w_gate.shape[2]
    swap = functools.partial(lax.ppermute, axis_name="section", perm=[(0, 1), (1, 0)])

    attn_pack = jnp.concatenate([w_query, w_key, w_value, w_out], axis=2)[0]
    mlp_pack = jnp.concatenate([w_gate, w_up, w_down], axis=2)[0]
    attn_all = lax.all_gather(attn_pack, ("section", "dp"), axis=0, tiled=True)
    mlp_all = lax.all_gather(mlp_pack, ("section", "dp"), axis=0, tiled=True)
    shard = norm_gains.shape[1]
    spread = lax.dynamic_update_slice(
        jnp.zeros((4, features), F32),
        norm_gains[0].astype(F32).T,
        (2 * section, lax.axis_index("dp") * shard),
    )
    all_gains = butterfly(spread, ("section", "dp"))
    weights = []
    gains = [all_gains[:2], all_gains[2:]]
    for layer in range(2):
        attn = attn_all[layer * features : (layer + 1) * features]
        mlp = mlp_all[layer * features : (layer + 1) * features]
        weights.append(
            (
                attn[:, : 3 * head_width],
                attn[:, 3 * head_width :],
                mlp[:, : 2 * units],
                mlp[:, 2 * units :],
            )
        )

    position = positions(own, devices)
    tables = [rotary_tables(position, theta) for theta in THETAS]
    length = lax.dynamic_index_in_dim(lengths, section, 0, keepdims=False)[0]
    scalars = jnp.stack([lax.axis_index("tensor").astype(jnp.int32), length.astype(jnp.int32)])

    resid = lax.dynamic_index_in_dim(inputs, section, 0, keepdims=False).astype(F32)
    residuals = []
    kept = []
    produced = []
    for layer in range(2):
        residuals.append(resid)
        result, saved = forward_layer(
            resid, weights[layer], gains[layer], layer == 0, tables[layer], scalars
        )
        kept.append(saved)
        produced.append(result.astype(BF16))
        resid = produced[-1].astype(F32)

    grad = lax.dynamic_index_in_dim(cotangent, section, 0, keepdims=False).astype(F32)
    sent_back = [None, None]
    attn_pieces = [None, None]
    mlp_pieces = [None, None]
    gain_grads = [None, None]
    for layer in (1, 0):
        d_resid, grad_attn, grad_mlp, gain_grads[layer] = backward_layer(
            grad,
            residuals[layer],
            kept[layer],
            weights[layer],
            gains[layer],
            layer == 0,
            tables[layer],
            scalars,
        )
        mlp_pieces[layer] = reduce_pack(grad_mlp)
        attn_pieces[layer] = reduce_pack(grad_attn)
        sent_back[layer] = d_resid.astype(BF16)
        grad = sent_back[layer].astype(F32)

    def by_layer(pair):
        mine = jnp.where(first, pair[0], pair[1])
        other = swap(jnp.where(first, pair[1], pair[0]))
        return jnp.stack([jnp.where(first, mine, other), jnp.where(first, other, mine)])[None]

    def whole(pair):
        mine = jnp.where(first, pair[0], pair[1])
        other = swap(jnp.where(first, pair[1], pair[0]))
        low = jnp.where(first, mine, other)
        high = jnp.where(first, other, mine)
        return jnp.concatenate([low, high], axis=1).astype(F32)[None]

    attn_grad = whole(attn_pieces)
    mlp_grad = whole(mlp_pieces)
    summed = butterfly(jnp.concatenate(gain_grads, axis=0), ("tensor", "section", "dp"))
    gain_grad = lax.dynamic_slice(
        summed, (2 * section, lax.axis_index("dp") * shard), (2, shard)
    ).T[None]
    return (
        by_layer(produced),
        by_layer(sent_back),
        attn_grad[:, :, :head_width],
        attn_grad[:, :, head_width : 2 * head_width],
        attn_grad[:, :, 2 * head_width : 3 * head_width],
        attn_grad[:, :, 3 * head_width :],
        mlp_grad[:, :, :units],
        mlp_grad[:, :, units : 2 * units],
        mlp_grad[:, :, 2 * units :],
        gain_grad,
    )


def solution(mesh):
    rows = P(None, ("dp", "tensor"), None)
    weight = P("section", "dp", "tensor")
    gain = P("section", "dp", None)
    out_rows = P("section", None, ("dp", "tensor"), None)
    return jax.shard_map(
        local_program,
        mesh=mesh,
        in_specs=(rows, P(None, "dp"), rows) + (weight,) * 7 + (gain,),
        out_specs=(out_rows, out_rows) + (weight,) * 7 + (gain,),
        check_vma=False,
    )
```
